32 devices in a mesh: row: 2 (over y), col: 16 (over z, x, core).
Axes of the slice: x: 2, y: 2, z: 4, core: 2. Of those that a mesh axis runs over, the one named last changes fastest.
Arguments:
- tokens: bfloat16 [512, 1024], P(('row', 'col')), may hold values from -6 to 6
- grad_out: bfloat16 [512, 1024], P(('row', 'col')), may hold values from -1.1953125 to 1.1953125
- gains: float32 [2, 1024], replicated, may hold values from 0.1 to 1.9
- flat_in: bfloat16 [16384, 2048], P(('row', 'col')), may hold values from -0.1875 to 0.1875
- flat_out: bfloat16 [16384, 2048], P(('row', 'col')), may hold values from -0.03125 to 0.03125
- flat_moment: float32 [2, 16384, 2048], P(None, ('row', 'col')), may hold values from -3 to 3
- flat_second: float32 [2, 16384, 2048], P(None, ('row', 'col')), may hold values from 0.05 to 2
- tile_in: bfloat16 [16, 6, 256, 2048], P('col', 'row'), may hold values from -0.1875 to 0.1875
- tile_out: bfloat16 [16, 6, 256, 2048], P('col', 'row'), may hold values from -0.03125 to 0.03125
- tile_moment: float32 [2, 16, 6, 256, 2048], P(None, 'col', 'row'), may hold values from -3 to 3
- tile_second: float32 [2, 16, 6, 256, 2048], P(None, 'col', 'row'), may hold values from 0.05 to 2
- owners: int32 [2, 16, 4], P(None, 'col'), may hold values from 0 to 1, as said below
Outputs:
- hidden_out: bfloat16 [512, 1024], P(('row', 'col'))
- grad_tokens: bfloat16 [512, 1024], P(('row', 'col'))
- new_flat_in: bfloat16 [16384, 2048], P(('row', 'col'))
- new_flat_out: bfloat16 [16384, 2048], P(('row', 'col'))
- new_flat_moment: float32 [2, 16384, 2048], P(None, ('row', 'col'))
- new_flat_second: float32 [2, 16384, 2048], P(None, ('row', 'col'))
- new_tile_in: bfloat16 [16, 6, 256, 2048], P('col', 'row')
- new_tile_out: bfloat16 [16, 6, 256, 2048], P('col', 'row')
- new_tile_moment: float32 [2, 16, 6, 256, 2048], P(None, 'col', 'row')
- new_tile_second: float32 [2, 16, 6, 256, 2048], P(None, 'col', 'row')
The draws below stay inside these ranges and needn't reach their ends.
Inputs may be any that keep to these rules, and one draw needn't show every extreme that they name: `owners`: for each matrix and column block, entry k names the row that owns tile k; each row owns at most 3 tiles of a block and matrix, and in each block and matrix some row owns exactly 3.
All inputs are finite; a program needn't handle non-finite values.
Results may differ from the reference program's by a relative error of at most 0.029.
Values may be sent and summed in bfloat16 or wider, within the bound.
A program may use at most 192 MiB of HBM per device.

```python
import math
import jax
import jax.numpy as jnp
from jax import lax

D = 1024
FF = 32768
OWN_CAP = 3
TOKENS = 512
GROUP_TOK = 256
BLOCK = 2048
TILES = 4
TILE_ROWS = 256
N_ROW = 2
N_COL = 16


def draw_owners(key, part):
    owner_pool = jnp.repeat(jnp.arange(N_ROW, dtype=jnp.int32), OWN_CAP)

    def one_block(sub_key):
        key_full, key_pick, key_order = jax.random.split(sub_key, 3)
        favored = jax.random.randint(key_full, (), 0, N_ROW, dtype=jnp.int32)
        scores = jax.random.permutation(key_pick, N_ROW * OWN_CAP).astype(jnp.int32) + jnp.where(owner_pool == favored, N_ROW * OWN_CAP, 0).astype(jnp.int32)
        picked = jnp.argsort(-scores, stable=True)[:2 * N_ROW]
        chosen = owner_pool[picked]
        return chosen[jax.random.permutation(key_order, 2 * N_ROW)]
    block_keys = jax.random.split(jax.random.fold_in(key, 17), 2 * N_COL)
    return jax.vmap(one_block)(block_keys).reshape(2, N_COL, 2 * N_ROW).astype(jnp.int32)


def block_levels(own_key, dims, cuts, least, high):
    factor_of, own = 1.0, jax.random.fold_in(own_key, 6)
    for position, shards_of in cuts:
        draws = jnp.exp(jax.random.uniform(jax.random.fold_in(own, position), (shards_of,), jnp.float32, least / len(cuts), high / len(cuts)))
        factor_of = factor_of * jnp.repeat(draws, dims[position] // shards_of).reshape([-1 if axis == position else 1 for axis in range(len(dims))])
    return factor_of


def bell_draw(rng, dims, deviation, reach, cuts=(), kind=jnp.bfloat16):
    drawn = jax.random.normal(rng, dims, jnp.float32) * deviation
    if len(cuts) > 0:
        drawn = block_levels(rng, dims, cuts, -0.22, 0.18) * drawn
    return jnp.clip(drawn, min=-reach, max=reach).astype(kind)


def setup_inputs(seed: int = 0) -> dict:
    streams_of = jax.random.split(jax.random.key(seed), 13)
    tokens = bell_draw(streams_of[0], (TOKENS, D), 1.0, 6.0, ((0, 32),))
    grad_out = bell_draw(streams_of[1], (TOKENS, D), 0.2, 1.1953125, ((0, 32),))
    gains = jnp.clip(1.0 + 0.18 * jax.random.normal(streams_of[2], (2, D), jnp.float32), 0.1, 1.9)
    flat_in = bell_draw(streams_of[3], (D * N_COL, BLOCK), D ** -0.5, 0.1875, ((0, 32),))
    flat_out = bell_draw(streams_of[4], (D * N_COL, BLOCK), FF ** -0.5, 0.03125, ((0, 32),))
    flat_moment = bell_draw(streams_of[5], (2, D * N_COL, BLOCK), 0.5, 3.0, ((1, 32),), jnp.float32)
    flat_second = jnp.clip(jnp.exp(math.log(2.0) - 3.6888794 * jax.random.uniform(streams_of[6], (2, D * N_COL, BLOCK), jnp.float32) ** block_levels(streams_of[6], (2, D * N_COL, BLOCK), ((1, 32),), -0.2, 0.2)), 0.05, 2.0)
    tile_in = bell_draw(streams_of[7], (N_COL, N_ROW * OWN_CAP, TILE_ROWS, BLOCK), D ** -0.5, 0.1875, ((0, 16), (1, 2)))
    tile_out = bell_draw(streams_of[8], (N_COL, N_ROW * OWN_CAP, TILE_ROWS, BLOCK), FF ** -0.5, 0.03125, ((0, 16), (1, 2)))
    tile_moment = bell_draw(streams_of[9], (2, N_COL, N_ROW * OWN_CAP, TILE_ROWS, BLOCK), 0.5, 3.0, ((1, 16), (2, 2)), jnp.float32)
    tile_second = jnp.clip(jnp.exp(math.log(2.0) - 3.6888794 * jax.random.uniform(streams_of[10], (2, N_COL, N_ROW * OWN_CAP, TILE_ROWS, BLOCK), jnp.float32) ** block_levels(streams_of[10], (2, N_COL, N_ROW * OWN_CAP, TILE_ROWS, BLOCK), ((1, 16), (2, 2)), -0.2, 0.2)), 0.05, 2.0)
    owners = draw_owners(jax.random.fold_in(streams_of[12], 71), 0)
    return dict(tokens=tokens, grad_out=grad_out, gains=gains, flat_in=flat_in, flat_out=flat_out, flat_moment=flat_moment, flat_second=flat_second, tile_in=tile_in, tile_out=tile_out, tile_moment=tile_moment, tile_second=tile_second, owners=owners)


norm_eps = 1e-06
beta_one = 0.9
beta_two = 0.95
learn_rate = 0.002
decay_rate = 0.1
adam_eps = 1e-08
gelu_coef = 0.7978845608

def gelu_value(hidden):
    tanh_term = jnp.tanh(gelu_coef * (hidden + 0.044715 * hidden * hidden * hidden))
    return 0.5 * hidden * (1.0 + tanh_term)

def gelu_slope(hidden):
    tanh_term = jnp.tanh(gelu_coef * (hidden + 0.044715 * hidden * hidden * hidden))
    return 0.5 * (1.0 + tanh_term) + 0.5 * hidden * (1.0 - tanh_term * tanh_term) * gelu_coef * (1.0 + 0.134145 * hidden * hidden)

def adam_update(weight, gradient, moment, second):
    new_moment = beta_one * moment + (1.0 - beta_one) * gradient
    new_second = beta_two * second + (1.0 - beta_two) * gradient * gradient
    weight_float = weight.astype(jnp.float32)
    stepped = weight_float - learn_rate * (new_moment / (jnp.sqrt(new_second) + adam_eps) + decay_rate * weight_float)
    return (stepped.astype(jnp.bfloat16), new_moment, new_second)

def slot_tables(owner_rows, slot_cap, row_total):
    tile_count = owner_rows.shape[-1]
    positions = jnp.arange(tile_count, dtype=jnp.int32)
    same_owner = owner_rows[..., :, None] == owner_rows[..., None, :]
    earlier = positions[None, :] < positions[:, None]
    tile_rank = lax.optimization_barrier(jnp.sum(jnp.where(same_owner & earlier, 1, 0), axis=-1)).astype(jnp.int32)
    slot_dest = (owner_rows * slot_cap + tile_rank).astype(jnp.int32)
    slot_ids = jnp.arange(row_total * slot_cap, dtype=jnp.int32)
    matches = slot_dest[..., None, :] == slot_ids[:, None]
    slot_tile = lax.optimization_barrier(jnp.sum(jnp.where(matches, positions, 0), axis=-1)).astype(jnp.int32)
    slot_live = jnp.any(matches, axis=-1)
    return (slot_dest, slot_tile, slot_live)

def layer_forward(layer_in, gain_vec, w_in, w_out):
    tok_float = layer_in.astype(jnp.float32)
    inv_rms = lax.rsqrt(lax.optimization_barrier(jnp.mean(tok_float * tok_float, axis=1, keepdims=True)) + norm_eps)
    normed = (tok_float * inv_rms * gain_vec).astype(jnp.bfloat16)
    hidden = jnp.dot(normed, w_in, preferred_element_type=jnp.float32)
    activated = gelu_value(hidden).astype(jnp.bfloat16)
    mixed_sum = lax.dot_general(activated, w_out, (((1,), (1,)), ((), ())), preferred_element_type=jnp.float32)
    return ((tok_float + mixed_sum).astype(jnp.bfloat16), (tok_float, inv_rms, normed, hidden, activated))

def group_sums(left_rows, right_rows):
    left_groups = left_rows.reshape(N_ROW, GROUP_TOK, left_rows.shape[1])
    right_groups = right_rows.reshape(N_ROW, GROUP_TOK, right_rows.shape[1])

    def add_group(running, operands):
        product = lax.dot_general(operands[0], operands[1], (((0,), (0,)), ((), ())), preferred_element_type=jnp.float32)
        rounded = lax.optimization_barrier(product.astype(jnp.bfloat16))
        return (running + rounded.astype(jnp.float32), None)
    start_sum = jnp.zeros((left_rows.shape[1], right_rows.shape[1]), jnp.float32)
    running, unused = lax.scan(add_group, start_sum, (left_groups, right_groups))
    return running

def layer_backward(cotangent, gain_vec, w_in, w_out, saved_state):
    tok_float, inv_rms, normed, hidden, activated = saved_state
    d_act = jnp.dot(cotangent, w_out, preferred_element_type=jnp.float32)
    d_hidden = (d_act * gelu_slope(hidden)).astype(jnp.bfloat16)
    d_normed = lax.dot_general(d_hidden, w_in, (((1,), (1,)), ((), ())), preferred_element_type=jnp.float32)
    gated = d_normed * gain_vec
    tok_grad = cotangent.astype(jnp.float32) + inv_rms * gated - tok_float * inv_rms * inv_rms * inv_rms * lax.optimization_barrier(jnp.mean(tok_float * gated, axis=1, keepdims=True))
    grad_in = group_sums(normed, d_hidden)
    grad_wout = group_sums(cotangent, activated)
    return (tok_grad.astype(jnp.bfloat16), grad_in, grad_wout)

def assemble(slot_data, slot_dest_m):
    tile_data = jnp.take_along_axis(slot_data, slot_dest_m[:, :, None, None], axis=1)
    return tile_data.transpose(1, 2, 0, 3).reshape(D, FF)

def tiled_update(slot_data, gradient, moment, second, slot_tile_m, slot_live_m):
    grad_tiles = gradient.reshape(TILES, TILE_ROWS, N_COL, BLOCK).transpose(2, 0, 1, 3)
    grad_slots = jnp.take_along_axis(grad_tiles, slot_tile_m[:, :, None, None], axis=1)
    new_weight, new_moment, new_second = adam_update(slot_data, grad_slots, moment, second)
    live_mask = slot_live_m[:, :, None, None]
    return (jnp.where(live_mask, new_weight, slot_data), jnp.where(live_mask, new_moment, moment), jnp.where(live_mask, new_second, second))

def reference(tokens, grad_out, gains, flat_in, flat_out, flat_moment, flat_second, tile_in, tile_out, tile_moment, tile_second, owners):
    slot_dest, slot_tile, slot_live = slot_tables(owners, OWN_CAP, N_ROW)
    first_in = flat_in.reshape(D, FF)
    first_out = flat_out.reshape(D, FF)
    second_in = assemble(tile_in, slot_dest[0])
    second_out = assemble(tile_out, slot_dest[1])
    middle, saved_one = layer_forward(tokens, gains[0], first_in, first_out)
    hidden_out, saved_two = layer_forward(middle, gains[1], second_in, second_out)
    grad_mid, grad_in_two, grad_out_two = layer_backward(grad_out, gains[1], second_in, second_out, saved_two)
    grad_tokens, grad_in_one, grad_out_one = layer_backward(grad_mid, gains[0], first_in, first_out, saved_one)
    new_flat_in, moment_in, second_in_f = adam_update(flat_in, grad_in_one.reshape(D * N_COL, BLOCK), flat_moment[0], flat_second[0])
    new_flat_out, moment_out, second_out_f = adam_update(flat_out, grad_out_one.reshape(D * N_COL, BLOCK), flat_moment[1], flat_second[1])
    new_tile_in, tmoment_in, tsecond_in = tiled_update(tile_in, grad_in_two, tile_moment[0], tile_second[0], slot_tile[0], slot_live[0])
    new_tile_out, tmoment_out, tsecond_out = tiled_update(tile_out, grad_out_two, tile_moment[1], tile_second[1], slot_tile[1], slot_live[1])
    return (hidden_out, grad_tokens, new_flat_in, new_flat_out, jnp.stack([moment_in, moment_out]), jnp.stack([second_in_f, second_out_f]), new_tile_in, new_tile_out, jnp.stack([tmoment_in, tmoment_out]), jnp.stack([tsecond_in, tsecond_out]))
```

```python
import jax
import jax.numpy as jnp
from jax import lax
from jax.experimental import pallas as pl
from jax.experimental.pallas import tpu as pltpu
from jax.sharding import PartitionSpec as P

norm_eps = 1e-06
beta_one = 0.9
beta_two = 0.95
learn_rate = 0.002
decay_rate = 0.1
adam_eps = 1e-08
gelu_coef = 0.7978845608
both = ("row", "col")


def gelu_both(hidden):
    square = hidden * hidden
    tanh_term = jnp.tanh(gelu_coef * (hidden + 0.044715 * square * hidden))
    value = 0.5 * hidden * (1.0 + tanh_term)
    slope = 0.5 * (1.0 + tanh_term) + 0.5 * hidden * (1.0 - tanh_term * tanh_term) * gelu_coef * (
        1.0 + 0.134145 * square
    )
    return value, slope


def adam_update(weight, gradient, moment, second):
    new_moment = beta_one * moment + (1.0 - beta_one) * gradient
    new_second = beta_two * second + (1.0 - beta_two) * gradient * gradient
    weight_float = weight.astype(jnp.float32)
    stepped = weight_float - learn_rate * (
        new_moment / (jnp.sqrt(new_second) + adam_eps) + decay_rate * weight_float
    )
    return (stepped.astype(jnp.bfloat16), new_moment, new_second)


def tile_ranks(owner_rows):
    positions = jnp.arange(owner_rows.shape[-1], dtype=jnp.int32)
    same_owner = owner_rows[..., :, None] == owner_rows[..., None, :]
    earlier = positions[None, :] < positions[:, None]
    return jnp.sum(jnp.where(same_owner & earlier, 1, 0), axis=-1).astype(jnp.int32)


def flat_kernel(w_in, w_out, g_in, g_out, mom, sec, o_in, o_out, o_mom, o_sec):
    for m, (w, g, o) in enumerate(((w_in, g_in, o_in), (w_out, g_out, o_out))):
        new = adam_update(w[...], g[...].astype(jnp.float32), mom[m], sec[m])
        o[...], o_mom[m], o_sec[m] = new


def flat_adam(w_in, w_out, g_in, g_out, mom, sec):
    rows, width = w_in.shape
    step = min(rows, 32)
    thin = pl.BlockSpec((step, width), lambda i: (i, 0))
    wide = pl.BlockSpec((2, step, width), lambda i: (0, i, 0))
    shape = jax.ShapeDtypeStruct
    return pl.pallas_call(
        flat_kernel,
        grid=(rows // step,),
        in_specs=[thin, thin, thin, thin, wide, wide],
        out_specs=[thin, thin, wide, wide],
        out_shape=[
            shape(w_in.shape, w_in.dtype),
            shape(w_out.shape, w_out.dtype),
            shape(mom.shape, mom.dtype),
            shape(sec.shape, sec.dtype),
        ],
        cost_estimate=pl.CostEstimate(
            flops=30 * mom.size, bytes_accessed=20 * mom.size + 2 * mom.size, transcendentals=mom.size
        ),
        name="flat_adam",
    )(w_in, w_out, g_in, g_out, mom, sec)


def tile_kernel(
    tiles, live, me, l_in, l_out, r_in, r_out, w_in, w_out, mom, sec, o_in, o_out, o_mom, o_sec
):
    slot = pl.program_id(0)
    parts = ((l_in, r_in, w_in, o_in), (l_out, r_out, w_out, o_out))
    for m, (left, right, w, o) in enumerate(parts):
        grad = jnp.dot(left[...], right[0], preferred_element_type=jnp.float32)
        alive = live[m, slot] > 0
        old_w, old_m, old_s = w[0, 0], mom[m, 0, 0], sec[m, 0, 0]
        new_w, new_m, new_s = adam_update(old_w, grad, old_m, old_s)
        o[0, 0] = jnp.where(alive, new_w.astype(jnp.float32), old_w.astype(jnp.float32)).astype(
            jnp.bfloat16
        )
        o_mom[m, 0, 0] = jnp.where(alive, new_m, old_m)
        o_sec[m, 0, 0] = jnp.where(alive, new_s, old_s)


def tile_adam(tiles, live, me, l_in, l_out, r_in, r_out, w_in, w_out, mom, sec):
    slot_cap, tile_rows, width = w_in.shape[1:]
    ranks, toks, sub = r_in.shape
    step = min(sub, 512)
    per = sub // step

    def left_map(m):
        return lambda s, h, tiles, live, me: (tiles[m, s], 0)

    def right_map(s, h, tiles, live, me):
        return (lax.rem(me[0] + ranks - h // per, ranks), 0, h % per)

    def thin_map(s, h, *unused):
        return (0, s, 0, h)

    def wide_map(s, h, *unused):
        return (0, 0, s, 0, h)

    right = pl.BlockSpec((1, toks, step), right_map)
    thin = pl.BlockSpec((1, 1, tile_rows, step), thin_map)
    wide = pl.BlockSpec((2, 1, 1, tile_rows, step), wide_map)
    shape = jax.ShapeDtypeStruct
    return pl.pallas_call(
        tile_kernel,
        grid_spec=pltpu.PrefetchScalarGridSpec(
            num_scalar_prefetch=3,
            grid=(slot_cap, width // step),
            in_specs=[
                pl.BlockSpec((tile_rows, toks), left_map(0)),
                pl.BlockSpec((tile_rows, toks), left_map(1)),
                right,
                right,
                thin,
                thin,
                wide,
                wide,
            ],
            out_specs=[thin, thin, wide, wide],
        ),
        out_shape=[
            shape(w_in.shape, w_in.dtype),
            shape(w_out.shape, w_out.dtype),
            shape(mom.shape, mom.dtype),
            shape(sec.shape, sec.dtype),
        ],
        cost_estimate=pl.CostEstimate(
            flops=2 * toks * mom.size, bytes_accessed=22 * mom.size, transcendentals=mom.size
        ),
        name="tile_adam",
    )(tiles, live, me, l_in, l_out, r_in, r_out, w_in, w_out, mom, sec)


def row_swap(pieces_for, row_total):
    got = [pieces_for(0)]
    for shift in range(1, row_total):
        pairs = [(src, (src + shift) % row_total) for src in range(row_total)]
        got.append(lax.ppermute(pieces_for(shift), "row", pairs))
    return jnp.stack(got)


def spread_sum(partial, total):
    toks, width = partial.shape
    sent = partial.astype(jnp.bfloat16)
    came = lax.all_to_all(sent, both, split_axis=0, concat_axis=0, tiled=True)
    return jnp.sum(came.reshape(total, toks // total, width).astype(jnp.float32), axis=0)


def late_sum(partial):
    return lax.psum_scatter(
        partial.astype(jnp.bfloat16), both, scatter_dimension=0, tiled=True
    ).astype(jnp.float32)


def dot_nt(left, right):
    return lax.dot_general(left, right, (((1,), (1,)), ((), ())), preferred_element_type=jnp.float32)


def dot_tn(left, right):
    return lax.dot_general(left, right, (((0,), (0,)), ((), ())), preferred_element_type=jnp.float32)


def norm_of(layer_in, gain_vec):
    tok_float = layer_in.astype(jnp.float32)
    inv_rms = lax.rsqrt(jnp.mean(tok_float * tok_float, axis=1, keepdims=True) + norm_eps)
    normed = (tok_float * inv_rms * gain_vec).astype(jnp.bfloat16)
    return tok_float, inv_rms, normed


def token_grad(cotangent, d_normed, gain_vec, tok_float, inv_rms):
    gated = d_normed * gain_vec
    return (
        cotangent.astype(jnp.float32)
        + inv_rms * gated
        - tok_float
        * inv_rms
        * inv_rms
        * inv_rms
        * jnp.mean(tok_float * gated, axis=1, keepdims=True)
    ).astype(jnp.bfloat16)


def shards(
    tokens,
    grad_out,
    gains,
    flat_in,
    flat_out,
    flat_moment,
    flat_second,
    tile_in,
    tile_out,
    tile_moment,
    tile_second,
    owners,
):
    row_total = lax.axis_size("row")
    col_total = lax.axis_size("col")
    total = row_total * col_total
    row_index = lax.axis_index("row")
    model_width = tokens.shape[1]
    block = flat_in.shape[1]
    sub = block // row_total
    own_rows = flat_in.shape[0] // col_total
    slot_cap = tile_in.shape[1]
    tile_rows = tile_in.shape[2]

    owner_rows = owners[:, 0, :]
    ranks = tile_ranks(owner_rows)
    came_from = lax.rem(row_index - owner_rows + row_total, row_total)
    slot_pick = came_from * slot_cap + ranks
    slots = jnp.arange(slot_cap, dtype=jnp.int32)[None, :, None]
    mine = (owner_rows == row_index)[:, None, :] & (ranks[:, None, :] == slots)
    positions = jnp.arange(owner_rows.shape[1], dtype=jnp.int32)
    my_tiles = jnp.sum(jnp.where(mine, positions, 0), axis=-1).astype(jnp.int32)
    my_live = jnp.any(mine, axis=-1).astype(jnp.int32)

    def flat_to_units(flat):
        parts = flat.reshape(own_rows, col_total, row_total, sub).transpose(2, 1, 0, 3)
        return lax.all_to_all(
            parts.reshape(total * own_rows, sub), both, split_axis=0, concat_axis=0, tiled=True
        )

    def units_to_flat(grad):
        came = lax.all_to_all(
            grad.astype(jnp.bfloat16), both, split_axis=0, concat_axis=0, tiled=True
        )
        parts = came.reshape(row_total, col_total, own_rows, sub).transpose(2, 1, 0, 3)
        return parts.reshape(own_rows * col_total, block)

    def tiles_to_units(tile, pick):
        def piece(shift):
            to_row = lax.rem(row_index + shift, row_total)
            return lax.dynamic_slice_in_dim(tile[0], to_row * sub, sub, 2)

        whole = row_swap(piece, row_total).reshape(row_total * slot_cap, tile_rows, sub)
        return jnp.take(whole, pick, axis=0).reshape(model_width, sub)

    def gather(x):
        return lax.all_gather(x, both, axis=0, tiled=True)

    tok_one, inv_one, normed_one = norm_of(tokens, gains[0])
    normed_one = gather(normed_one)
    one_in = flat_to_units(flat_in)
    one_out = flat_to_units(flat_out)
    cot_two = gather(grad_out)
    two_in = tiles_to_units(tile_in, slot_pick[0])
    two_out = tiles_to_units(tile_out, slot_pick[1])
    hidden_one = jnp.dot(normed_one, one_in, preferred_element_type=jnp.float32)
    act_one, slope_one = gelu_both(hidden_one)
    act_one = act_one.astype(jnp.bfloat16)
    middle = (tok_one + spread_sum(dot_nt(act_one, one_out), total)).astype(jnp.bfloat16)

    tok_two, inv_two, normed_two = norm_of(middle, gains[1])
    normed_two = gather(normed_two)
    hidden_two = jnp.dot(normed_two, two_in, preferred_element_type=jnp.float32)
    act_two, slope_two = gelu_both(hidden_two)
    act_two = act_two.astype(jnp.bfloat16)
    d_act_two = jnp.dot(cot_two, two_out, preferred_element_type=jnp.float32)
    d_hidden_two = (d_act_two * slope_two).astype(jnp.bfloat16)
    d_normed_two = spread_sum(dot_nt(d_hidden_two, two_in), total)
    grad_mid = token_grad(grad_out, d_normed_two, gains[1], tok_two, inv_two)
    cot_one = gather(grad_mid)

    d_act_one = jnp.dot(cot_one, one_out, preferred_element_type=jnp.float32)
    d_hidden_one = (d_act_one * slope_one).astype(jnp.bfloat16)
    flat_grad_in = units_to_flat(dot_tn(normed_one, d_hidden_one))
    flat_grad_out = units_to_flat(dot_tn(cot_one, act_one))

    act_late, _ = lax.optimization_barrier((act_two, cot_one))
    mixed_two = late_sum(dot_nt(act_late, two_out))
    hidden_out = (tok_two + mixed_two).astype(jnp.bfloat16)
    d_normed_one = late_sum(dot_nt(d_hidden_one, one_in))
    grad_tokens = token_grad(grad_mid, d_normed_one, gains[0], tok_one, inv_one)

    d_hidden_rows = row_swap(lambda shift: d_hidden_two, row_total)
    act_rows = row_swap(lambda shift: act_two, row_total)
    new_tile = tile_adam(
        my_tiles,
        my_live,
        row_index.astype(jnp.int32).reshape(1),
        normed_two.T,
        cot_two.T,
        d_hidden_rows,
        act_rows,
        tile_in,
        tile_out,
        tile_moment,
        tile_second,
    )
    new_flat = flat_adam(flat_in, flat_out, flat_grad_in, flat_grad_out, flat_moment, flat_second)
    return (hidden_out, grad_tokens, *new_flat, *new_tile)


def solution(mesh):
    return jax.shard_map(
        shards,
        mesh=mesh,
        in_specs=(
            P(("row", "col"), None),
            P(("row", "col"), None),
            P(),
            P(("row", "col"), None),
            P(("row", "col"), None),
            P(None, ("row", "col"), None),
            P(None, ("row", "col"), None),
            P("col", "row", None, None),
            P("col", "row", None, None),
            P(None, "col", "row", None, None),
            P(None, "col", "row", None, None),
            P(None, "col", None),
        ),
        out_specs=(
            P(("row", "col"), None),
            P(("row", "col"), None),
            P(("row", "col"), None),
            P(("row", "col"), None),
            P(None, ("row", "col"), None),
            P(None, ("row", "col"), None),
            P("col", "row", None, None),
            P("col", "row", None, None),
            P(None, "col", "row", None, None),
            P(None, "col", "row", None, None),
        ),
        check_vma=False,
    )
```
